128 devices in a mesh: row: 16 (over y, x_lo, core), col: 8 (over z, x_hi).
Axes of the slice: x: 4 (x_hi: 2, x_lo: 2; x = x_hi * 2 + x_lo), y: 4, z: 4, core: 2. Of those that a mesh axis runs over, the one named last changes fastest.
Arguments:
- density: bfloat16 [16384, 16384], P('col', 'row'), may hold values from -0.0625 to 0.0625
- hamiltonian: bfloat16 [16384, 16384], P('row', 'col'), may hold values from -6 to 6
- pattern_p: int32 [128, 128], P('col', 'row'), may hold values 0 or 1
- pattern_h: int32 [128, 128], P('row', 'col'), may hold values 0 or 1
- pattern_s: int32 [16, 128], P('col', 'row'), may hold values 0 or 1
- owner: int32 [8, 16, 16, 1], P('col', 'row'), may hold values from 0 to 7; in each aligned block of 16 rows (0 to 15, 16 to 31, ..., all dimensions but the last counted through in order) at most 4 rows name the same one
- d_intersection: bfloat16 [16, 8, 3, 32, 128, 128], P('row', 'col'), may hold values from -6 to 6
- d_hamilton: bfloat16 [16, 8, 3, 32, 128, 128], P('row', 'col'), may hold values from -6 to 6
Outputs:
- weighted: bfloat16 [2048, 16384], P('col', 'row')
- forces: float32 [16, 8, 3, 32], P('row', 'col')
The draws below stay inside these ranges and needn't reach their ends.
Inputs may be any that keep to these rules, and one draw needn't show every extreme that they name: Among the 16 blocks of one device no owner is named more than 4 times.
All inputs are finite; a program needn't handle non-finite values. No bound on the sum of `pattern_p` or of `pattern_h` or of `pattern_s` on one device may be relied on, other than what follows from the above.
Results may differ from the reference program's by a relative error of at most 0.0049.
Values may be sent and summed in bfloat16 or wider, within the bound.
No kernel may reach another device: no remote copies, remote signals or barrier semaphores. Data moves between devices by JAX's collectives and lax.ppermute only.
A program may use at most 128 MiB of HBM per device.

```python
import math
import jax
import jax.numpy as jnp
import numpy as np

BLOCK = 128
CBLK = 8
SBLK = 2
NB = 128
N = 16384
MB = 16
M = 2048
CAP = 4
SLOTS = 32
N_ROW = 16
N_COL = 8


def touch_ends(drawn, key, low, high):
    shape = drawn.shape
    index_at = [jax.random.randint(jax.random.fold_in(key, axis), (), 0, shape[axis]) for axis in range(len(shape))]
    drawn = drawn.at[tuple(index_at)].set(low)
    longest = shape.index(max(shape))
    index_at[longest] = (index_at[longest] + 1) % shape[longest]
    return drawn.at[tuple(index_at)].set(high)


def level_of(rng, extent, split, low, top_value):
    def one(dim, parts):
        steps = jax.random.uniform(jax.random.fold_in(jax.random.fold_in(rng, 6), dim), (parts,), jnp.float32, low / len(split), top_value / len(split))
        return jnp.repeat(jnp.exp(steps), extent[dim] // parts).reshape((-1,) + (1,) * (len(extent) - dim - 1))

    level = one(*split[0])
    for cut in split[1:]:
        level = level * one(*cut)
    return level


def routed_block(own_key, own, number, rows, amount, top, bound, skew):
    order = jax.random.permutation(own_key, amount)
    heavy_load, ordinary = shares(amount, rows * top, bound, skew, True), shares(amount, rows * top, bound, skew, False)
    places = jnp.arange(amount)

    def named(lengths, turn):
        used = int((lengths > 0).sum())
        fixed = max(1, used // 4)
        shifted = fixed + (places - fixed + turn * (used - fixed)) % max(1, amount - fixed)
        return jnp.zeros((amount,), jnp.int32).at[order[jnp.where(places < fixed, places, shifted)]].set(jnp.asarray(lengths, jnp.int32))

    lengths = jnp.where(number % 4 == 0, named(heavy_load, number // 4), named(ordinary, number - number // 4 - 1))
    mixed = jax.random.permutation(jax.random.fold_in(own, 3), amount)
    giver, taker = mixed[0:amount // 2 * 2:2], mixed[1:amount // 2 * 2:2]
    room = jnp.minimum(lengths[giver] - 1, bound - lengths[taker]) // 2
    room = jnp.where((giver == order[0]) | (taker == order[0]) | (lengths[taker] == 0), 0, jnp.maximum(room, 0))
    shifted = jax.random.randint(jax.random.fold_in(own, 4), (amount // 2,), 0, 1 << 20) % (room + 1)
    lengths = lengths.at[giver].add(-shifted).at[taker].add(shifted)
    labels = jnp.searchsorted(jnp.cumsum(lengths), jnp.arange(rows * top), side="right").astype(jnp.int32)
    listing = labels.reshape(top, rows).T
    listing = listing[jax.random.permutation(jax.random.fold_in(own, 1), rows)]
    turn = jax.random.randint(jax.random.fold_in(own, 2), (rows, 1), 0, top)
    return jnp.take_along_axis(listing, (jnp.arange(top)[None, :] + turn) % top, axis=1)


def shares(number_of, total, reach, slope, full):
    portions = [(1 << 20) // math.isqrt(standing ** slope) + 1 for standing in range(1, number_of + 1)]
    largest = reach if full else min(reach, max(-(-total // number_of), total * portions[0] // sum(portions)))
    least = 1 if total - largest >= number_of - 1 else 0
    counts, rest = [largest] + [least] * (number_of - 1), total - largest - least * (number_of - 1)
    while rest > 0:
        free = [i for i in range(1, number_of) if counts[i] < largest] or [i for i in range(1, number_of) if counts[i] < reach]
        whole, remaining = sum([portions[i] for i in free]), rest
        for i in free:
            extra = min(reach - counts[i], max(1, remaining * portions[i] // whole), rest)
            counts[i] = counts[i] + extra
            rest = rest - extra
    return np.array(counts)


def noise(own_key, shape, width, most, pieces=(), kind=jnp.bfloat16):
    drawn = width * jax.random.normal(own_key, shape, jnp.float32)
    if pieces:
        drawn = drawn * level_of(own_key, shape, pieces, -0.22, 0.18)
    return jnp.clip(drawn, -most, most).astype(kind)


def setup_inputs(seed: int = 0) -> dict:
    splits = jax.random.split(jax.random.key(seed), 9)
    density = noise(splits[0], (N, N), (N // 2) ** -0.5, 0.0625, ((0, 8), (1, 16)))
    hamiltonian = noise(splits[1], (N, N), 1.0, 6.0, ((0, 16), (1, 8)))
    pattern_p = touch_ends((jax.random.randint(splits[2], (NB, NB), 0, 2) < 1).astype(jnp.int32), jax.random.fold_in(splits[2], 1), 0, 1)
    pattern_h = touch_ends((jax.random.randint(splits[3], (NB, NB), 0, 2) < 1).astype(jnp.int32), jax.random.fold_in(splits[3], 1), 0, 1)
    pattern_s = touch_ends((jax.random.randint(splits[4], (MB, NB), 0, 2) < 1).astype(jnp.int32), jax.random.fold_in(splits[4], 1), 0, 1)
    owner_keys = jax.random.split(jax.random.fold_in(splits[5], 1), N_COL * N_ROW * (SBLK * CBLK) // (SBLK * CBLK))
    owner_turns = jax.random.permutation(jax.random.fold_in(splits[5], 3), N_COL * N_ROW * (SBLK * CBLK) // (SBLK * CBLK))
    owner = jax.vmap(lambda own, number: routed_block(jax.random.fold_in(splits[5], 2), own, number, SBLK * CBLK, N_COL, 1, CAP, 2))(owner_keys, owner_turns).reshape((N_COL, N_ROW, SBLK * CBLK, 1))
    d_intersection = noise(splits[6], (N_ROW, N_COL, 3, SLOTS, BLOCK, BLOCK), 1.0, 6.0, ((0, 16), (1, 8)))
    d_hamilton = noise(splits[7], (N_ROW, N_COL, 3, SLOTS, BLOCK, BLOCK), 1.0, 6.0, ((0, 16), (1, 8)))
    return dict(density=density, hamiltonian=hamiltonian, pattern_p=pattern_p, pattern_h=pattern_h, pattern_s=pattern_s, owner=owner, d_intersection=d_intersection, d_hamilton=d_hamilton)


def spread(matrix, pattern):
    rows, cols = matrix.shape
    rb, cb = pattern.shape
    tiles = matrix.reshape(rb, rows // rb, cb, cols // cb) * pattern[:, None, :, None].astype(matrix.dtype)
    return tiles.reshape(rows, cols)


def to_blocks(matrix):
    tiles = matrix.reshape(N_COL, SBLK, BLOCK, N_ROW, CBLK, BLOCK).transpose(3, 0, 1, 4, 2, 5)
    return tiles.reshape(N_ROW, N_COL, SBLK * CBLK, BLOCK * BLOCK).astype(jnp.float32)


def reference(density, hamiltonian, pattern_p, pattern_h, pattern_s, owner, d_intersection, d_hamilton):
    masked_p = spread(density, pattern_p)
    masked_h = spread(hamiltonian, pattern_h)
    slab = masked_p.reshape(N_COL, N // N_COL, N)[:, : SBLK * BLOCK, :].reshape(M, N)
    panel = jnp.dot(slab, masked_h, preferred_element_type=jnp.float32).astype(jnp.bfloat16)
    product = jnp.dot(panel, masked_p, preferred_element_type=jnp.float32)
    weighted = spread(product, pattern_s).astype(jnp.bfloat16)
    w_blocks = to_blocks(weighted)
    p_blocks = to_blocks(slab)
    target = owner.transpose(1, 0, 2, 3).reshape(N_ROW, N_COL, SBLK * CBLK)
    onehot = (target[..., None] == jnp.arange(N_COL, dtype=jnp.int32)).astype(jnp.int32)
    before = jnp.cumsum(onehot, axis=2) - onehot
    rank = jnp.sum(before * onehot, axis=3)
    slot_id = target * CAP + rank
    select = (slot_id[..., None] == jnp.arange(SLOTS, dtype=jnp.int32)).astype(jnp.float32)

    def route(blocks):
        sent = jnp.einsum("rcks,rckx->rcsx", select, blocks)
        sent = sent.reshape(N_ROW, N_COL, N_COL, CAP, BLOCK * BLOCK).transpose(0, 2, 1, 3, 4)
        return sent.reshape(N_ROW, N_COL, SLOTS, BLOCK * BLOCK)

    got_w = route(w_blocks)
    got_p = route(p_blocks)
    dov = d_intersection.astype(jnp.float32).reshape(N_ROW, N_COL, 3, SLOTS, BLOCK * BLOCK)
    dham = d_hamilton.astype(jnp.float32).reshape(N_ROW, N_COL, 3, SLOTS, BLOCK * BLOCK)
    first = jnp.einsum("rdzsx,rdsx->rdzs", dham, got_p)
    second = jnp.einsum("rdzsx,rdsx->rdzs", dov, got_w)
    forces = (first - second) / BLOCK
    return weighted, forces
```

```python
import functools

import jax
import jax.numpy as jnp
from jax import lax
from jax.experimental import pallas as pl
from jax.experimental.pallas import tpu as pltpu
from jax.sharding import Mesh, PartitionSpec as P

BLOCK = 128
CBLK = 8
SBLK = 2
BF = jnp.bfloat16
F32 = jnp.float32
WIRE = jnp.float16
EARLY = (0, 1, 2, 6)
LATE = (3, 7, 4, 5)
ROW = ("y", "xlo", "core")
COL = ("z", "xhi")


def ring_ops(axis, swap):
    n = lax.axis_size(axis)
    up = [(i, (i + 1) % n) for i in range(n)]
    down = [(i, (i - 1) % n) for i in range(n)]
    flip = [(0, 1), (1, 0)]
    return (
        lambda v: lax.ppermute(v, axis, up),
        lambda v: lax.ppermute(v, axis, down),
        lambda v: lax.ppermute(v, swap, flip),
    )


def gather_tree(piece, ops):
    up, down, flip = ops
    side = flip(piece)
    up_own = up(piece)
    down_own = down(piece)
    down_side = down(side)
    up_two = up(up_own)
    up_side = up(side)
    down_two = down(down_side)
    return [piece, side, down_own, down_side, up_two, down_two, up_own, up_side]


PAD = 16
TOP = 115.0


def level_of(value):
    peak = jnp.maximum(jnp.max(jnp.abs(value)), 2.0**-100)
    return jnp.ceil(jnp.log2(peak)) + 101.0


def encode(value, level):
    scaled = value * jnp.exp2(TOP - level)
    return lax.pad(scaled, level, ((0, PAD, 0), (0, 0, 0))).astype(WIRE)


def decode(packed):
    rows = packed.shape[0] - PAD
    level = packed[rows, 0].astype(F32)
    return packed[:rows].astype(F32) * jnp.exp2(level - TOP), level


def scatter_tree(part, level, ops):
    up, down, flip = ops
    r1m = down(encode(part[4], level))
    r1p = up(encode(part[5], level))
    r3m = down(encode(part[7], level))
    r3p = up(encode(part[2], level))
    v1m, l1m = decode(r1m)
    v1p, l1p = decode(r1p)
    r2m = down(encode(part[6] + v1m, jnp.maximum(level, l1m) + 1.0))
    r2p = up(encode(part[3] + v1p, jnp.maximum(level, l1p) + 1.0))
    v3m, l3m = decode(r3m)
    v2p, l2p = decode(r2p)
    rx = flip(encode(part[1] + v3m + v2p, jnp.maximum(jnp.maximum(level, l3m), l2p) + 2.0))
    return part[0] + decode(r3p)[0] + decode(r2m)[0] + decode(rx)[0]


def other_core(v):
    return lax.ppermute(v, "core", [(0, 1), (1, 0)])


def h_body(index, pattern, src, dst):
    first = index[0]
    for g in range(CBLK):
        col = index[g + 1]
        cols = pl.ds(pl.multiple_of((col - first) * BLOCK, BLOCK), BLOCK)
        for row in range(CBLK):
            rows = pl.ds(row * BLOCK, BLOCK)
            value = src[rows, cols]
            keep = pattern[row, col] != 0
            dst[rows, g * BLOCK : (g + 1) * BLOCK] = jnp.where(keep, value, jnp.zeros_like(value))


def mask_h(ham, pattern, half, group):
    rows = ham.shape[0]
    width = CBLK * BLOCK
    index = jnp.concatenate((jnp.full((1,), half * CBLK, jnp.int32), half * CBLK + group))
    return pl.pallas_call(
        h_body,
        out_shape=jax.ShapeDtypeStruct((rows, width), BF),
        grid_spec=pltpu.PrefetchScalarGridSpec(
            num_scalar_prefetch=2,
            grid=(1,),
            in_specs=[pl.BlockSpec((rows, width), lambda g, idx, pat: (0, idx[0] // CBLK))],
            out_specs=pl.BlockSpec((rows, width), lambda g, idx, pat: (0, 0)),
        ),
        name="mask_h",
    )(index, pattern, ham)


def p_body(index, pattern, src, dst):
    first = index[0]
    for g in range(dst.shape[0] // BLOCK):
        row = index[g + 1]
        rows = pl.ds(pl.multiple_of((row - first) * BLOCK, BLOCK), BLOCK)
        for col in range(CBLK):
            cols = pl.ds(col * BLOCK, BLOCK)
            value = src[rows, cols]
            keep = pattern[row, col] != 0
            dst[g * BLOCK : (g + 1) * BLOCK, cols] = jnp.where(keep, value, jnp.zeros_like(value))


def mask_p(den, pattern, start, rows_in):
    height = rows_in.shape[0] * BLOCK
    cols = den.shape[1]
    index = jnp.concatenate((jnp.full((1,), start, jnp.int32), rows_in))
    return pl.pallas_call(
        p_body,
        out_shape=jax.ShapeDtypeStruct((height, cols), BF),
        grid_spec=pltpu.PrefetchScalarGridSpec(
            num_scalar_prefetch=2,
            grid=(1,),
            in_specs=[pl.BlockSpec((height, cols), lambda g, idx, pat: (idx[0] * BLOCK // height, 0))],
            out_specs=pl.BlockSpec((height, cols), lambda g, idx, pat: (0, 0)),
        ),
        name="mask_p",
    )(index, pattern, den)


def pick_body(source, blocks, out):
    for slot in range(out.shape[0]):
        k = source[slot]
        safe = jnp.maximum(k, 0)
        rows = pl.ds(pl.multiple_of((safe // CBLK) * BLOCK, BLOCK), BLOCK)
        cols = pl.ds(pl.multiple_of((safe % CBLK) * BLOCK, BLOCK), BLOCK)
        value = blocks[rows, cols]
        out[slot] = jnp.where(k >= 0, value, jnp.zeros_like(value))


def pick(blocks, source):
    slots = source.shape[0]
    return pl.pallas_call(
        pick_body,
        out_shape=jax.ShapeDtypeStruct((slots, BLOCK, BLOCK), BF),
        in_specs=[
            pl.BlockSpec(memory_space=pltpu.SMEM),
            pl.BlockSpec(memory_space=pltpu.VMEM),
        ],
        out_specs=pl.BlockSpec(memory_space=pltpu.VMEM),
        name="pick",
    )(source, blocks)


def routing(owner, columns, slot_total):
    capacity = slot_total // columns
    target = owner.reshape(SBLK * CBLK)
    onehot = (target[:, None] == jnp.arange(columns, dtype=jnp.int32)[None, :]).astype(jnp.int32)
    before = jnp.cumsum(onehot, axis=0) - onehot
    rank = jnp.sum(before * onehot, axis=1)
    slot_id = target * capacity + rank
    hit = slot_id[None, :] == jnp.arange(slot_total, dtype=jnp.int32)[:, None]
    number = jnp.arange(SBLK * CBLK, dtype=jnp.int32)[None, :] + 1
    return jnp.sum(jnp.where(hit, number, 0), axis=1) - 1


def pair_sums(derivative, blocks):
    return jnp.sum(derivative.astype(F32) * blocks.astype(F32)[None], axis=(2, 3))


def local(density, hamiltonian, pattern_p, pattern_h, pattern_s, owner, d_intersection, d_hamilton):
    y, xlo, core = (lax.axis_index(a) for a in ROW)
    columns = lax.axis_size(COL)
    slot_total = d_intersection.shape[3]
    y_ops = ring_ops("y", "xlo")
    z_ops = ring_ops("z", "xhi")

    step = jnp.arange(CBLK, dtype=jnp.int32)
    group = ((y + step // 2) % 4) * 2 + (xlo ^ (step % 2))
    mine, theirs = core * CBLK, (1 - core) * CBLK

    slab = mask_p(density, pattern_p, 0, jnp.arange(SBLK, dtype=jnp.int32))
    h_other = other_core(mask_h(hamiltonian, pattern_h, 1 - core, group))
    h_mine = mask_h(hamiltonian, pattern_h, core, group)
    p_mine = mask_p(density, pattern_p, mine, mine + group)
    p_other = mask_p(density, pattern_p, theirs, theirs + group)

    source = routing(owner, columns, slot_total)
    d_over = d_intersection.reshape(d_intersection.shape[2:])
    d_ham = d_hamilton.reshape(d_hamilton.shape[2:])

    def route(blocks):
        return lax.all_to_all(pick(blocks, source), COL, split_axis=0, concat_axis=0, tiled=True)

    pieces = gather_tree(slab, z_ops)
    products = {}
    peak = None
    for number, chosen in enumerate((EARLY, LATE)):
        rows = jnp.concatenate([pieces[k] for k in chosen], axis=0)
        other = other_core(rows)
        part = jnp.dot(rows, h_mine, preferred_element_type=F32) + jnp.dot(
            other, h_other, preferred_element_type=F32
        )
        if number == 0:
            slab_late, part = lax.optimization_barrier((slab, part))
            routed_slab = route(slab_late)
        parts = [part[:, g * BLOCK : (g + 1) * BLOCK] for g in range(CBLK)]
        panel = scatter_tree(parts, level_of(part), y_ops).astype(BF)
        cols = jnp.concatenate(gather_tree(panel, y_ops), axis=1)
        other = other_core(cols)
        product = jnp.dot(cols, p_mine, preferred_element_type=F32) + jnp.dot(
            other, p_other, preferred_element_type=F32
        )
        level = level_of(product)
        peak = level if peak is None else jnp.maximum(peak, level)
        for at, k in enumerate(chosen):
            products[k] = product[at * SBLK * BLOCK : (at + 1) * SBLK * BLOCK]
    product = scatter_tree([products[k] for k in range(CBLK)], peak, z_ops)
    keep = jnp.repeat(jnp.repeat(pattern_s, BLOCK, axis=0), BLOCK, axis=1).astype(F32)
    weighted = (product * keep).astype(BF)

    first = pair_sums(d_ham, routed_slab)
    second = pair_sums(d_over, route(weighted))
    forces = (first - second) / BLOCK
    return weighted, forces.reshape((1, 1) + forces.shape)


def solution(mesh):
    fine = Mesh(mesh.devices.reshape(4, 2, 2, 4, 2), ROW + COL)
    in_specs = (
        P(COL, ROW),
        P(ROW, COL),
        P(COL, ROW),
        P(ROW, COL),
        P(COL, ROW),
        P(COL, ROW, None, None),
        P(ROW, COL, None, None, None, None),
        P(ROW, COL, None, None, None, None),
    )
    out_specs = (P(COL, ROW), P(ROW, COL, None, None))
    return jax.shard_map(local, mesh=fine, in_specs=in_specs, out_specs=out_specs, check_vma=False)
```

```python
import functools

import jax
import jax.numpy as jnp
from jax import lax
from jax.experimental import pallas as pl
from jax.experimental.pallas import tpu as pltpu
from jax.sharding import Mesh, PartitionSpec as P

BLOCK = 128
CBLK = 8
SBLK = 2
BF = jnp.bfloat16
F32 = jnp.float32
WIRE = jnp.float16
ROW = ("y", "xlo", "core")
COL = ("z", "xhi")
ROW_PAIR = ("y", "xlo")
EARLY = (0, 1, 2, 6)
LATE = (3, 7, 4, 5)
PAD = 16
TOP = 115.0


def exchange(pieces, axes):
    return lax.all_to_all(pieces, axes, split_axis=0, concat_axis=0, tiled=True)


def flip(v, axis):
    return lax.ppermute(v, axis, [(0, 1), (1, 0)])


def gather_direct(piece, axes):
    return exchange(jnp.broadcast_to(piece[None], (CBLK,) + piece.shape), axes)


def shifted(v, k):
    dz, dx = k // 2, k % 2
    nz, nx = lax.axis_size("z"), lax.axis_size("xhi")
    pairs = [
        (z * nx + x, (z + dz) % nz * nx + (x ^ dx)) for z in range(nz) for x in range(nx)
    ]
    return lax.ppermute(v, COL, pairs)


def level_of(peak):
    return jnp.ceil(jnp.log2(jnp.maximum(jnp.max(peak), 2.0**-100))) + 101.0


def encode(padded, peak):
    level = level_of(peak)
    row = lax.broadcasted_iota(jnp.int32, padded.shape, 1)
    rows = padded.shape[1] - PAD
    return jnp.where(row < rows, padded * jnp.exp2(TOP - level), level).astype(WIRE)


def decode_sum(packed):
    rows = packed.shape[1] - PAD
    factor = jnp.exp2(packed[:, rows, 0].astype(F32) - TOP)[:, None, None]
    total = jnp.sum(packed[:, :rows].astype(F32) * factor, axis=0)
    return total, jnp.max(packed[:, rows, 0].astype(F32))


def other_core(v):
    return flip(v, "core")


def mask_body(corner, pattern, src, dst):
    rows, cols = (size // BLOCK for size in src.shape)
    for row in range(rows):
        for col in range(cols):
            at = (slice(row * BLOCK, (row + 1) * BLOCK), slice(col * BLOCK, (col + 1) * BLOCK))
            keep = pattern[corner[0] * rows + row, corner[1] * cols + col] != 0

            @pl.when(keep)
            def _():
                dst[at] = src[at]

            @pl.when(jnp.logical_not(keep))
            def _():
                dst[at] = jnp.zeros((BLOCK, BLOCK), BF)


def slab_body(target, pattern, src, dst):
    rows, cols = src.shape
    mask_body((0, 0), pattern, src, dst.at[:rows])
    lane = lax.broadcasted_iota(jnp.int32, (PAD, cols), 1)
    note = jnp.zeros((PAD, cols), F32)
    for k in range(SBLK * CBLK):
        note = jnp.where(lane == k, target[k].astype(F32), note)
    dst[rows:] = note.astype(BF)


def call_mask(body, scalars, matrix, shape, height, index):
    return pl.pallas_call(
        body,
        out_shape=jax.ShapeDtypeStruct((height, shape[1]), BF),
        grid_spec=pltpu.PrefetchScalarGridSpec(
            num_scalar_prefetch=2,
            grid=(1,),
            in_specs=[pl.BlockSpec(shape, index)],
            out_specs=pl.BlockSpec((height, shape[1]), lambda g, at, pat: (0, 0)),
        ),
        name=body.__name__,
    )(*scalars, matrix)


def mask(matrix, pattern, shape, row, col):
    corner = jnp.stack((jnp.asarray(row, jnp.int32), jnp.asarray(col, jnp.int32)))
    index = lambda g, at, pat: (at[0], at[1])
    return call_mask(mask_body, (corner, pattern), matrix, shape, shape[0], index)


def mask_slab(matrix, pattern, target, shape):
    index = lambda g, at, pat: (0, 0)
    return call_mask(slab_body, (target, pattern), matrix, shape, shape[0] + PAD, index)


def h_dot_body(*refs):
    count = (len(refs) - 4) // 2
    mine, other = refs[:count], refs[count : 2 * count]
    w_mine, w_other, out, peak = refs[2 * count :]
    height = mine[0].shape[0] - PAD
    tops = []
    for at in range(count):
        values = jnp.dot(mine[at][:height], w_mine[...], preferred_element_type=F32)
        values += jnp.dot(other[at][:height], w_other[...], preferred_element_type=F32)
        for g in range(out.shape[0]):
            out[g, at * height : (at + 1) * height] = values[:, g * BLOCK : (g + 1) * BLOCK]
        tops.append(jnp.max(jnp.abs(values), axis=0, keepdims=True))
    for g in range(out.shape[0]):
        out[g, count * height :] = jnp.zeros((PAD, BLOCK), F32)
    peak[0] = jnp.broadcast_to(functools.reduce(jnp.maximum, tops), peak.shape[1:])


def p_dot_body(mine, other, w_mine, w_other, out):
    def flat(tiles):
        return jnp.concatenate([tiles[g] for g in range(CBLK)], axis=1)

    values = jnp.dot(flat(mine), w_mine[...], preferred_element_type=F32)
    values += jnp.dot(flat(other), w_other[...], preferred_element_type=F32)
    out[...] = values


COST = pl.CostEstimate(flops=1 << 20, bytes_accessed=1 << 20, transcendentals=0)
ROOM = pltpu.CompilerParams(vmem_limit_bytes=58 << 20)


def dot_specs(operands, width):
    whole = [pl.BlockSpec(v.shape, lambda n, rank=v.ndim: (0,) * rank) for v in operands]
    return whole + [pl.BlockSpec((width, 2 * BLOCK), lambda n: (0, n))] * 2


def h_dot(mine, other, w_mine, w_other):
    width = w_mine.shape[0]
    tile = 2 * BLOCK
    steps = width // tile
    return pl.pallas_call(
        h_dot_body,
        out_shape=(
            jax.ShapeDtypeStruct((CBLK, width + PAD, BLOCK), F32),
            jax.ShapeDtypeStruct((steps, 8, tile), F32),
        ),
        grid=(steps,),
        in_specs=dot_specs(mine + other, width),
        out_specs=(
            pl.BlockSpec((2, width + PAD, BLOCK), lambda n: (n, 0, 0)),
            pl.BlockSpec((1, 8, tile), lambda n: (n, 0, 0)),
        ),
        cost_estimate=COST,
        compiler_params=ROOM,
        name="h_dot",
    )(*mine, *other, w_mine, w_other)


def p_dot(mine, other, w_mine, w_other):
    width = w_mine.shape[0]
    tile = 2 * BLOCK
    return pl.pallas_call(
        p_dot_body,
        out_shape=jax.ShapeDtypeStruct((width, width), F32),
        grid=(width // tile,),
        in_specs=dot_specs((mine, other), width),
        out_specs=pl.BlockSpec((width, tile), lambda n: (0, n)),
        cost_estimate=COST,
        compiler_params=ROOM,
        name="p_dot",
    )(mine, other, w_mine, w_other)


def collect_body(source, base, *refs):
    pieces, out = refs[:-1], refs[-1]
    room = source.shape[1]
    for k, blocks in enumerate(pieces):
        for q in range(room):
            b = source[k, q]
            safe = jnp.maximum(b, 0)
            rows = pl.ds(pl.multiple_of((safe // CBLK) * BLOCK, BLOCK), BLOCK)
            cols = pl.ds(pl.multiple_of((safe % CBLK) * BLOCK, BLOCK), BLOCK)
            value = blocks[rows, cols]
            out[base[k] * room + q] = jnp.where(b >= 0, value, jnp.zeros_like(value))


def collect(pieces, source, base):
    scalar = pl.BlockSpec(memory_space=pltpu.SMEM)
    whole = pl.BlockSpec(memory_space=pltpu.VMEM)
    slots = source.shape[0] * source.shape[1]
    return pl.pallas_call(
        collect_body,
        out_shape=jax.ShapeDtypeStruct((slots, BLOCK, BLOCK), BF),
        in_specs=[scalar, scalar] + [whole] * len(pieces),
        out_specs=whole,
        compiler_params=pltpu.CompilerParams(vmem_limit_bytes=24 << 20),
        name="collect",
    )(source, base, *pieces)


def pick_body(source, blocks, out):
    for slot in range(out.shape[0]):
        k = source[slot]
        safe = jnp.maximum(k, 0)
        rows = pl.ds(pl.multiple_of((safe // CBLK) * BLOCK, BLOCK), BLOCK)
        cols = pl.ds(pl.multiple_of((safe % CBLK) * BLOCK, BLOCK), BLOCK)
        value = blocks[rows, cols]
        out[slot] = jnp.where(k >= 0, value, jnp.zeros_like(value))


def pick(blocks, source):
    slots = source.shape[0]
    return pl.pallas_call(
        pick_body,
        out_shape=jax.ShapeDtypeStruct((slots, BLOCK, BLOCK), BF),
        in_specs=[
            pl.BlockSpec(memory_space=pltpu.SMEM),
            pl.BlockSpec(memory_space=pltpu.VMEM),
        ],
        out_specs=pl.BlockSpec(memory_space=pltpu.VMEM),
        name="pick",
    )(source, blocks)


def routing(target, columns, capacity):
    count = target.shape[0]
    onehot = (target[:, None] == jnp.arange(columns, dtype=jnp.int32)[None, :]).astype(jnp.int32)
    place = jnp.arange(count, dtype=jnp.int32)
    earlier = (place[None, :] < place[:, None]).astype(jnp.int32)
    rank = jnp.sum(earlier * (target[None, :] == target[:, None]), axis=1)
    hit = (rank[:, None, None] == jnp.arange(capacity, dtype=jnp.int32)) & (onehot[:, :, None] > 0)
    return jnp.sum(jnp.where(hit, place[:, None, None] + 1, 0), axis=0) - 1


def pair_sums(derivative, blocks):
    return jnp.sum(derivative.astype(F32) * blocks.astype(F32)[None], axis=(2, 3))


def local(density, hamiltonian, pattern_p, pattern_h, pattern_s, owner, d_intersection, d_hamilton):
    core = lax.axis_index("core")
    columns = lax.axis_size(COL)
    slot_total = d_intersection.shape[3]
    width = CBLK * BLOCK

    capacity = slot_total // columns
    target = owner.reshape(SBLK * CBLK)
    source = routing(target, columns, capacity).reshape(slot_total)
    d_over = d_intersection.reshape(d_intersection.shape[2:])
    d_ham = d_hamilton.reshape(d_hamilton.shape[2:])

    def route(blocks):
        return exchange(pick(blocks, source), COL)

    slab = mask_slab(density, pattern_p[:SBLK], target, (SBLK * BLOCK, width))
    up, down = ([(i, (i + d) % 4) for i in range(4)] for d in (1, -1))
    barrier = lax.optimization_barrier
    height = SBLK * BLOCK
    side = flip(slab, "xhi")
    up_own = lax.ppermute(slab, "z", up)
    down_own = lax.ppermute(slab, "z", down)
    h_mine = mask(hamiltonian, pattern_h, (width, width), 0, core)
    h_sent = mask(hamiltonian, pattern_h, (width, width), 0, 1 - core)
    side, up_own, down_own, h_mine, h_sent = barrier((side, up_own, down_own, h_mine, h_sent))
    h_other = other_core(h_sent)
    down_side = lax.ppermute(side, "z", down)
    up_two = lax.ppermute(up_own, "z", up)
    up_side = lax.ppermute(side, "z", up)
    pieces = [slab, side, down_own, down_side, up_two, None, up_own, up_side]

    def partial_w(tiles, p_mine, p_other):
        part = p_dot(tiles, other_core(tiles), p_mine, p_other)
        blocks = [part[at * height : (at + 1) * height] for at in range(len(EARLY))]
        return blocks[0], [(v * scale).astype(WIRE) for v in blocks]

    mine = [pieces[k] for k in EARLY]
    others, down_side = barrier(([other_core(v) for v in mine], down_side))
    pieces[3] = down_side
    pieces[5] = lax.ppermute(down_side, "z", down)
    partial, peak = h_dot(mine, others, h_mine, h_other)
    packed, late, density = barrier(
        (encode(partial, peak), [pieces[k] for k in LATE], density)
    )
    for k, piece in zip(LATE, late):
        pieces[k] = piece
    mine = [pieces[k] for k in LATE]
    packed_late = encode(*h_dot(mine, [other_core(v) for v in mine], h_mine, h_other))
    arrived, packed_late = barrier((exchange(packed, ROW_PAIR), packed_late))
    arrived_late = exchange(packed_late, ROW_PAIR)
    panel, level = decode_sum(arrived)
    panel = panel.astype(BF)
    copies = jnp.broadcast_to(panel[None], (CBLK,) + panel.shape)
    keep = jnp.repeat(jnp.repeat(pattern_s, BLOCK, axis=0), BLOCK, axis=1).astype(F32)
    p_mine = mask(density, pattern_p, (width, width), core, 0)
    p_other = mask(density, pattern_p, (width, width), 1 - core, 0)
    most_p = jnp.max(jnp.abs(density)).astype(F32)
    copies, arrived_late, p_mine, p_other, keep, most_p = barrier(
        (copies, arrived_late, p_mine, p_other, keep, most_p)
    )
    panel_late, level_late = decode_sum(arrived_late)
    panel_late = panel_late.astype(BF)
    copies_late = jnp.broadcast_to(panel_late[None], (CBLK,) + panel_late.shape)
    room = jnp.ceil(jnp.log2(jnp.maximum(most_p, 2.0**-100))) + 14.0
    room = jnp.full((8, BLOCK), room + jnp.maximum(level, level_late), F32)
    two = [(i, (i + 2) % 4) for i in range(4)]
    room = jnp.maximum(room, other_core(room))
    room = jnp.maximum(room, lax.ppermute(room, "z", two))
    room = jnp.maximum(room, lax.ppermute(room, "z", up))
    room = jnp.max(jnp.maximum(room, flip(room, "xhi"))) - 101.0
    tiles, copies_late, room = barrier((exchange(copies, ROW_PAIR), copies_late, room))
    tiles_late = exchange(copies_late, ROW_PAIR)
    scale, unscale = jnp.exp2(14.0 - room), jnp.exp2(room - 14.0)

    early, wire = partial_w(tiles, p_mine, p_other)
    wire, tiles_late = barrier((wire, tiles_late))
    _, wire_late = partial_w(tiles_late, p_mine, p_other)
    total = early
    for part, chosen in ((wire, EARLY), (wire_late, LATE)):
        for v, k in zip(part, chosen):
            if k:
                total = total + shifted(v, k).astype(F32) * unscale
        if k == EARLY[-1]:
            total = barrier(total)
    weighted = (total * keep).astype(BF)

    z, xhi = lax.axis_index("z"), lax.axis_index("xhi")
    step = jnp.arange(CBLK, dtype=jnp.int32)
    base = ((z + step // 2) % 4) * 2 + (xhi ^ (step % 2))
    owners = jnp.stack([p[height, : SBLK * CBLK] for p in pieces]).astype(jnp.int32)
    me = z * 2 + xhi
    found = jax.vmap(lambda t: routing(t, columns, capacity))(owners)
    mine = jnp.sum(jnp.where(jnp.arange(columns)[None, :, None] == me, found, 0), axis=1)
    routed_slab = collect(pieces, mine, base)

    first = pair_sums(d_ham, routed_slab)
    second = pair_sums(d_over, route(weighted))
    forces = (first - second) / BLOCK
    return weighted, forces.reshape((1, 1) + forces.shape)


def solution(mesh):
    fine = Mesh(mesh.devices.reshape(4, 2, 2, 4, 2), ROW + COL)
    in_specs = (
        P(COL, ROW),
        P(ROW, COL),
        P(COL, ROW),
        P(ROW, COL),
        P(COL, ROW),
        P(COL, ROW, None, None),
        P(ROW, COL, None, None, None, None),
        P(ROW, COL, None, None, None, None),
    )
    out_specs = (P(COL, ROW), P(ROW, COL, None, None))
    return jax.shard_map(local, mesh=fine, in_specs=in_specs, out_specs=out_specs, check_vma=False)
```

```python
import functools

import jax
import jax.numpy as jnp
from jax import lax
from jax.experimental import pallas as pl
from jax.experimental.pallas import tpu as pltpu
from jax.sharding import Mesh, PartitionSpec as P

BLOCK = 128
CBLK = 8
SBLK = 2
BF = jnp.bfloat16
F32 = jnp.float32
WIRE = jnp.float16
ROW = ("y", "xlo", "core")
COL = ("z", "xhi")
ROW_PAIR = ("y", "xlo")
EARLY = (0, 1, 2, 6)
LATE = (3, 7, 4, 5)
PAD = 16
TOP = 115.0


def exchange(pieces, axes):
    return lax.all_to_all(pieces, axes, split_axis=0, concat_axis=0, tiled=True)


def flip(v, axis):
    return lax.ppermute(v, axis, [(0, 1), (1, 0)])


def gather_direct(piece, axes):
    return exchange(jnp.broadcast_to(piece[None], (CBLK,) + piece.shape), axes)


def shifted(v, k):
    dz, dx = k // 2, k % 2
    nz, nx = lax.axis_size("z"), lax.axis_size("xhi")
    pairs = [
        (z * nx + x, (z + dz) % nz * nx + (x ^ dx)) for z in range(nz) for x in range(nx)
    ]
    return lax.ppermute(v, COL, pairs)


def level_of(peak):
    return jnp.ceil(jnp.log2(jnp.maximum(jnp.max(peak), 2.0**-100))) + 101.0


def encode(padded, peak):
    level = level_of(peak)
    row = lax.broadcasted_iota(jnp.int32, padded.shape, 1)
    rows = padded.shape[1] - PAD
    return jnp.where(row < rows, padded * jnp.exp2(TOP - level), level).astype(WIRE)


def decode_sum(packed):
    rows = packed.shape[1] - PAD
    factor = jnp.exp2(packed[:, rows, 0].astype(F32) - TOP)[:, None, None]
    total = jnp.sum(packed[:, :rows].astype(F32) * factor, axis=0)
    return total, jnp.max(packed[:, rows, 0].astype(F32))


def other_core(v):
    return flip(v, "core")


def mask_body(corner, pattern, src, dst):
    rows, cols = (size // BLOCK for size in src.shape)
    for row in range(rows):
        for col in range(cols):
            at = (slice(row * BLOCK, (row + 1) * BLOCK), slice(col * BLOCK, (col + 1) * BLOCK))
            keep = pattern[corner[0] * rows + row, corner[1] * cols + col] != 0

            @pl.when(keep)
            def _():
                dst[at] = src[at]

            @pl.when(jnp.logical_not(keep))
            def _():
                dst[at] = jnp.zeros((BLOCK, BLOCK), BF)


def slab_body(target, pattern, src, dst):
    rows, cols = src.shape
    mask_body((0, 0), pattern, src, dst.at[:rows])
    lane = lax.broadcasted_iota(jnp.int32, (PAD, cols), 1)
    note = jnp.zeros((PAD, cols), F32)
    for k in range(SBLK * CBLK):
        note = jnp.where(lane == k, target[k].astype(F32), note)
    dst[rows:] = note.astype(BF)


def call_mask(body, scalars, matrix, shape, height, index):
    return pl.pallas_call(
        body,
        out_shape=jax.ShapeDtypeStruct((height, shape[1]), BF),
        grid_spec=pltpu.PrefetchScalarGridSpec(
            num_scalar_prefetch=2,
            grid=(1,),
            in_specs=[pl.BlockSpec(shape, index)],
            out_specs=pl.BlockSpec((height, shape[1]), lambda g, at, pat: (0, 0)),
        ),
        name=body.__name__,
    )(*scalars, matrix)


def mask(matrix, pattern, shape, row, col):
    corner = jnp.stack((jnp.asarray(row, jnp.int32), jnp.asarray(col, jnp.int32)))
    index = lambda g, at, pat: (at[0], at[1])
    return call_mask(mask_body, (corner, pattern), matrix, shape, shape[0], index)


def mask_slab(matrix, pattern, target, shape):
    index = lambda g, at, pat: (0, 0)
    return call_mask(slab_body, (target, pattern), matrix, shape, shape[0] + PAD, index)


def h_dot_body(*refs):
    count = (len(refs) - 4) // 2
    mine, other = refs[:count], refs[count : 2 * count]
    w_mine, w_other, out, peak = refs[2 * count :]
    height = mine[0].shape[0] - PAD
    tops = []
    for at in range(count):
        values = jnp.dot(mine[at][:height], w_mine[...], preferred_element_type=F32)
        values += jnp.dot(other[at][:height], w_other[...], preferred_element_type=F32)
        for g in range(out.shape[0]):
            out[g, at * height : (at + 1) * height] = values[:, g * BLOCK : (g + 1) * BLOCK]
        tops.append(jnp.max(jnp.abs(values), axis=0, keepdims=True))
    for g in range(out.shape[0]):
        out[g, count * height :] = jnp.zeros((PAD, BLOCK), F32)
    peak[0] = jnp.broadcast_to(functools.reduce(jnp.maximum, tops), peak.shape[1:])


def p_dot_body(mine, other, w_mine, w_other, out):
    def flat(tiles):
        return jnp.concatenate([tiles[g] for g in range(CBLK)], axis=1)

    values = jnp.dot(flat(mine), w_mine[...], preferred_element_type=F32)
    values += jnp.dot(flat(other), w_other[...], preferred_element_type=F32)
    out[...] = values


COST = pl.CostEstimate(flops=1 << 20, bytes_accessed=1 << 20, transcendentals=0)
ROOM = pltpu.CompilerParams(vmem_limit_bytes=58 << 20)


def dot_specs(operands, width):
    whole = [pl.BlockSpec(v.shape, lambda n, rank=v.ndim: (0,) * rank) for v in operands]
    return whole + [pl.BlockSpec((width, 2 * BLOCK), lambda n: (0, n))] * 2


def h_dot(mine, other, w_mine, w_other):
    width = w_mine.shape[0]
    tile = 2 * BLOCK
    steps = width // tile
    return pl.pallas_call(
        h_dot_body,
        out_shape=(
            jax.ShapeDtypeStruct((CBLK, width + PAD, BLOCK), F32),
            jax.ShapeDtypeStruct((steps, 8, tile), F32),
        ),
        grid=(steps,),
        in_specs=dot_specs(mine + other, width),
        out_specs=(
            pl.BlockSpec((2, width + PAD, BLOCK), lambda n: (n, 0, 0)),
            pl.BlockSpec((1, 8, tile), lambda n: (n, 0, 0)),
        ),
        cost_estimate=COST,
        compiler_params=ROOM,
        name="h_dot",
    )(*mine, *other, w_mine, w_other)


def p_dot(mine, other, w_mine, w_other):
    width = w_mine.shape[0]
    tile = 2 * BLOCK
    return pl.pallas_call(
        p_dot_body,
        out_shape=jax.ShapeDtypeStruct((width, width), F32),
        grid=(width // tile,),
        in_specs=dot_specs((mine, other), width),
        out_specs=pl.BlockSpec((width, tile), lambda n: (0, n)),
        cost_estimate=COST,
        compiler_params=ROOM,
        name="p_dot",
    )(mine, other, w_mine, w_other)


def collect_body(source, base, *refs):
    pieces, out = refs[:-1], refs[-1]
    room = source.shape[1]
    for k, blocks in enumerate(pieces):
        for q in range(room):
            b = source[k, q]
            safe = jnp.maximum(b, 0)
            rows = pl.ds(pl.multiple_of((safe // CBLK) * BLOCK, BLOCK), BLOCK)
            cols = pl.ds(pl.multiple_of((safe % CBLK) * BLOCK, BLOCK), BLOCK)
            value = blocks[rows, cols]
            out[base[k] * room + q] = jnp.where(b >= 0, value, jnp.zeros_like(value))


def collect(pieces, source, base):
    scalar = pl.BlockSpec(memory_space=pltpu.SMEM)
    whole = pl.BlockSpec(memory_space=pltpu.VMEM)
    slots = source.shape[0] * source.shape[1]
    return pl.pallas_call(
        collect_body,
        out_shape=jax.ShapeDtypeStruct((slots, BLOCK, BLOCK), BF),
        in_specs=[scalar, scalar] + [whole] * len(pieces),
        out_specs=whole,
        compiler_params=pltpu.CompilerParams(vmem_limit_bytes=24 << 20),
        name="collect",
    )(source, base, *pieces)


def pick_body(source, blocks, out):
    for slot in range(out.shape[0]):
        k = source[slot]
        safe = jnp.maximum(k, 0)
        rows = pl.ds(pl.multiple_of((safe // CBLK) * BLOCK, BLOCK), BLOCK)
        cols = pl.ds(pl.multiple_of((safe % CBLK) * BLOCK, BLOCK), BLOCK)
        value = blocks[rows, cols]
        out[slot] = jnp.where(k >= 0, value, jnp.zeros_like(value))


def pick(blocks, source):
    slots = source.shape[0]
    return pl.pallas_call(
        pick_body,
        out_shape=jax.ShapeDtypeStruct((slots, BLOCK, BLOCK), BF),
        in_specs=[
            pl.BlockSpec(memory_space=pltpu.SMEM),
            pl.BlockSpec(memory_space=pltpu.VMEM),
        ],
        out_specs=pl.BlockSpec(memory_space=pltpu.VMEM),
        name="pick",
    )(source, blocks)


def routing(target, columns, capacity):
    count = target.shape[0]
    onehot = (target[:, None] == jnp.arange(columns, dtype=jnp.int32)[None, :]).astype(jnp.int32)
    place = jnp.arange(count, dtype=jnp.int32)
    earlier = (place[None, :] < place[:, None]).astype(jnp.int32)
    rank = jnp.sum(earlier * (target[None, :] == target[:, None]), axis=1)
    hit = (rank[:, None, None] == jnp.arange(capacity, dtype=jnp.int32)) & (onehot[:, :, None] > 0)
    return jnp.sum(jnp.where(hit, place[:, None, None] + 1, 0), axis=0) - 1


def pair_sums(derivative, blocks):
    return jnp.sum(derivative.astype(F32) * blocks.astype(F32)[None], axis=(2, 3))


def local(density, hamiltonian, pattern_p, pattern_h, pattern_s, owner, d_intersection, d_hamilton):
    core = lax.axis_index("core")
    columns = lax.axis_size(COL)
    slot_total = d_intersection.shape[3]
    width = CBLK * BLOCK

    capacity = slot_total // columns
    target = owner.reshape(SBLK * CBLK)
    source = routing(target, columns, capacity).reshape(slot_total)
    d_over = d_intersection.reshape(d_intersection.shape[2:])
    d_ham = d_hamilton.reshape(d_hamilton.shape[2:])

    def route(blocks):
        return exchange(pick(blocks, source), COL)

    slab = mask_slab(density, pattern_p[:SBLK], target, (SBLK * BLOCK, width))
    up, down = ([(i, (i + d) % 4) for i in range(4)] for d in (1, -1))
    barrier = lax.optimization_barrier
    height = SBLK * BLOCK
    side = flip(slab, "xhi")
    up_own = lax.ppermute(slab, "z", up)
    down_own = lax.ppermute(slab, "z", down)
    h_mine = mask(hamiltonian, pattern_h, (width, width), 0, core)
    h_sent = mask(hamiltonian, pattern_h, (width, width), 0, 1 - core)
    side, up_own, down_own, h_mine, h_sent = barrier((side, up_own, down_own, h_mine, h_sent))
    h_other = other_core(h_sent)
    down_side = lax.ppermute(side, "z", down)
    up_two = lax.ppermute(up_own, "z", up)
    up_side = lax.ppermute(side, "z", up)
    pieces = [slab, side, down_own, down_side, up_two, None, up_own, up_side]

    mine = [pieces[k] for k in EARLY]
    partial, peak = h_dot(mine, [other_core(v) for v in mine], h_mine, h_other)
    peak, down_side_late = barrier((peak, down_side))
    packed, down_side, up_two, up_side, density = barrier(
        (encode(partial, peak), down_side, up_two, up_side, density)
    )
    pieces[3], pieces[4], pieces[7] = down_side, up_two, up_side
    pieces[5] = lax.ppermute(down_side_late, "z", down)
    mine = [pieces[k] for k in LATE]
    packed_late = encode(*h_dot(mine, [other_core(v) for v in mine], h_mine, h_other))
    arrived, packed_late = barrier((exchange(packed, ROW_PAIR), packed_late))
    arrived_late = exchange(packed_late, ROW_PAIR)
    panel, level = decode_sum(arrived)
    panel = panel.astype(BF)
    copies = jnp.broadcast_to(panel[None], (CBLK,) + panel.shape)
    keep = jnp.repeat(jnp.repeat(pattern_s, BLOCK, axis=0), BLOCK, axis=1).astype(F32)
    p_mine = mask(density, pattern_p, (width, width), core, 0)
    p_other = mask(density, pattern_p, (width, width), 1 - core, 0)
    most_p = jnp.max(jnp.abs(density)).astype(F32)
    copies, arrived_late, p_mine, p_other, keep, most_p = barrier(
        (copies, arrived_late, p_mine, p_other, keep, most_p)
    )
    panel_late, level_late = decode_sum(arrived_late)
    panel_late = panel_late.astype(BF)
    copies_late = jnp.broadcast_to(panel_late[None], (CBLK,) + panel_late.shape)
    room = jnp.ceil(jnp.log2(jnp.maximum(most_p, 2.0**-100))) + 14.0
    room = jnp.full((8, BLOCK), room + jnp.maximum(level, level_late), F32)
    two = [(i, (i + 2) % 4) for i in range(4)]
    room = jnp.maximum(room, other_core(room))
    room = jnp.maximum(room, lax.ppermute(room, "z", two))
    room = jnp.maximum(room, lax.ppermute(room, "z", up))
    room = jnp.max(jnp.maximum(room, flip(room, "xhi"))) - 101.0
    room = jnp.maximum(room, -100.0)
    tiles_late, copies, room = barrier((exchange(copies_late, ROW_PAIR), copies, room))
    tiles = exchange(copies, ROW_PAIR)
    scale, unscale = jnp.exp2(14.0 - room), jnp.exp2(room - 14.0)

    part_late = p_dot(tiles_late, other_core(tiles_late), p_mine, p_other)
    blocks = {k: part_late[at * height : (at + 1) * height] * scale for at, k in enumerate(LATE)}
    near, far = lax.ppermute(blocks[4].astype(WIRE), "z", down), lax.ppermute(
        blocks[5].astype(WIRE), "z", up
    )
    tiles, near, far = barrier((tiles, near, far))
    got = [
        shifted(blocks[7].astype(WIRE), 7),
        shifted((blocks[3] + far.astype(F32)).astype(WIRE), 3),
    ]
    part = p_dot(tiles, other_core(tiles), p_mine, p_other)
    total, one, two, six = (part[at * height : (at + 1) * height] * scale for at in range(4))
    wires = [v.astype(WIRE) for v in (one, two, six + near.astype(F32))]
    total, wires = barrier((total, wires))
    got = [shifted(v, k) for v, k in zip(wires, (1, 2, 6))] + got
    for v in got:
        total = total + v.astype(F32)
    total = total * unscale
    weighted = (total * keep).astype(BF)

    z, xhi = lax.axis_index("z"), lax.axis_index("xhi")
    step = jnp.arange(CBLK, dtype=jnp.int32)
    base = ((z + step // 2) % 4) * 2 + (xhi ^ (step % 2))
    owners = jnp.stack([p[height, : SBLK * CBLK] for p in pieces]).astype(jnp.int32)
    me = z * 2 + xhi
    found = jax.vmap(lambda t: routing(t, columns, capacity))(owners)
    mine = jnp.sum(jnp.where(jnp.arange(columns)[None, :, None] == me, found, 0), axis=1)
    routed_slab = collect(pieces, mine, base)

    first = pair_sums(d_ham, routed_slab)
    second = pair_sums(d_over, route(weighted))
    forces = (first - second) / BLOCK
    return weighted, forces.reshape((1, 1) + forces.shape)


def solution(mesh):
    fine = Mesh(mesh.devices.reshape(4, 2, 2, 4, 2), ROW + COL)
    in_specs = (
        P(COL, ROW),
        P(ROW, COL),
        P(COL, ROW),
        P(ROW, COL),
        P(COL, ROW),
        P(COL, ROW, None, None),
        P(ROW, COL, None, None, None, None),
        P(ROW, COL, None, None, None, None),
    )
    out_specs = (P(COL, ROW), P(ROW, COL, None, None))
    return jax.shard_map(local, mesh=fine, in_specs=in_specs, out_specs=out_specs, check_vma=False)
```

```python
import functools

import jax
import jax.numpy as jnp
from jax import lax
from jax.experimental import pallas as pl
from jax.experimental.pallas import tpu as pltpu
from jax.sharding import Mesh, PartitionSpec as P

BLOCK = 128
CBLK = 8
SBLK = 2
BF = jnp.bfloat16
F32 = jnp.float32
WIRE = jnp.float16
ROW = ("y", "xlo", "core")
COL = ("z", "xhi")
ROW_PAIR = ("y", "xlo")
EARLY = (0, 1, 2, 6)
LATE = (3, 7, 4, 5)
PAD = 16
TOP = 115.0


def exchange(pieces, axes):
    return lax.all_to_all(pieces, axes, split_axis=0, concat_axis=0, tiled=True)


def flip(v, axis):
    return lax.ppermute(v, axis, [(0, 1), (1, 0)])


def gather_direct(piece, axes):
    return exchange(jnp.broadcast_to(piece[None], (CBLK,) + piece.shape), axes)


def shifted(v, k):
    dz, dx = k // 2, k % 2
    nz, nx = lax.axis_size("z"), lax.axis_size("xhi")
    pairs = [
        (z * nx + x, (z + dz) % nz * nx + (x ^ dx)) for z in range(nz) for x in range(nx)
    ]
    return lax.ppermute(v, COL, pairs)


def level_of(peak):
    return jnp.ceil(jnp.log2(jnp.maximum(jnp.max(peak), 2.0**-100))) + 101.0


def encode(padded, peak):
    level = level_of(peak)
    row = lax.broadcasted_iota(jnp.int32, padded.shape, 1)
    rows = padded.shape[1] - PAD
    return jnp.where(row < rows, padded * jnp.exp2(TOP - level), level).astype(WIRE)


def decode_sum(packed):
    rows = packed.shape[1] - PAD
    factor = jnp.exp2(packed[:, rows, 0].astype(F32) - TOP)[:, None, None]
    total = jnp.sum(packed[:, :rows].astype(F32) * factor, axis=0)
    return total, jnp.max(packed[:, rows, 0].astype(F32))


def other_core(v):
    return flip(v, "core")


def keep_rows(pattern, row, col, src, dst):
    rows, cols = (size // BLOCK for size in src.shape)
    at_col = lax.broadcasted_iota(jnp.int32, (1, src.shape[1]), 1) // BLOCK
    for r in range(rows):
        keep = jnp.zeros((1, src.shape[1]), F32)
        for c in range(cols):
            keep = jnp.where(at_col == c, pattern(row + r, col + c).astype(F32), keep)
        at = slice(r * BLOCK, (r + 1) * BLOCK)
        dst[at] = src[at] * keep.astype(BF)


def mask_body(corner, pattern, src, dst):
    rows, cols = (size // BLOCK for size in src.shape)
    read = lambda r, c: pattern[r, c]
    keep_rows(read, corner[0] * rows, corner[1] * cols, src, dst)


def turned_body(corner, pattern, src, dst):
    rows, cols = (size // BLOCK for size in src.shape)
    read = lambda r, c: pattern[c, r]
    keep_rows(read, corner[0] * rows, corner[1] * cols, src, dst)


def slab_body(target, pattern, src, dst):
    rows, cols = src.shape
    keep_rows(lambda r, c: pattern[c, r], 0, 0, src, dst.at[:rows])
    lane = lax.broadcasted_iota(jnp.int32, (PAD, cols), 1)
    note = jnp.zeros((PAD, cols), F32)
    for k in range(SBLK * CBLK):
        note = jnp.where(lane == k, target[k].astype(F32), note)
    dst[rows:] = note.astype(BF)


def call_mask(body, scalars, matrix, shape, height, index):
    return pl.pallas_call(
        body,
        out_shape=jax.ShapeDtypeStruct((height, shape[1]), BF),
        grid_spec=pltpu.PrefetchScalarGridSpec(
            num_scalar_prefetch=2,
            grid=(1,),
            in_specs=[pl.BlockSpec(shape, index)],
            out_specs=pl.BlockSpec((height, shape[1]), lambda g, at, pat: (0, 0)),
        ),
        name=body.__name__,
    )(*scalars, matrix)


def mask(body, matrix, pattern, shape, row, col):
    corner = jnp.stack((jnp.asarray(row, jnp.int32), jnp.asarray(col, jnp.int32)))
    index = lambda g, at, pat: (at[0], at[1])
    return call_mask(body, (corner, pattern), matrix, shape, shape[0], index)


def mask_slab(matrix, pattern, target, shape):
    index = lambda g, at, pat: (0, 0)
    return call_mask(slab_body, (target, pattern), matrix, shape, shape[0] + PAD, index)


def h_dot_body(*refs):
    count = (len(refs) - 4) // 2
    mine, other = refs[:count], refs[count : 2 * count]
    w_mine, w_other, out, peak = refs[2 * count :]
    height = mine[0].shape[0] - PAD
    tops = []
    for at in range(count):
        values = jnp.dot(mine[at][:height], w_mine[...], preferred_element_type=F32)
        values += jnp.dot(other[at][:height], w_other[...], preferred_element_type=F32)
        for g in range(out.shape[0]):
            out[g, at * height : (at + 1) * height] = values[:, g * BLOCK : (g + 1) * BLOCK]
        tops.append(jnp.max(jnp.abs(values), axis=0, keepdims=True))
    for g in range(out.shape[0]):
        out[g, count * height :] = jnp.zeros((PAD, BLOCK), F32)
    peak[0] = jnp.broadcast_to(functools.reduce(jnp.maximum, tops), peak.shape[1:])


def p_dot_body(mine, other, w_mine, w_other, out):
    def flat(tiles):
        return jnp.concatenate([tiles[g] for g in range(CBLK)], axis=1)

    values = jnp.dot(flat(mine), w_mine[...], preferred_element_type=F32)
    values += jnp.dot(flat(other), w_other[...], preferred_element_type=F32)
    out[...] = values


COST = pl.CostEstimate(flops=1 << 20, bytes_accessed=1 << 20, transcendentals=0)
ROOM = pltpu.CompilerParams(vmem_limit_bytes=58 << 20)


def dot_specs(operands, width):
    whole = [pl.BlockSpec(v.shape, lambda n, rank=v.ndim: (0,) * rank) for v in operands]
    return whole + [pl.BlockSpec((width, 2 * BLOCK), lambda n: (0, n))] * 2


def h_dot(mine, other, w_mine, w_other):
    width = w_mine.shape[0]
    tile = 2 * BLOCK
    steps = width // tile
    return pl.pallas_call(
        h_dot_body,
        out_shape=(
            jax.ShapeDtypeStruct((CBLK, width + PAD, BLOCK), F32),
            jax.ShapeDtypeStruct((steps, 8, tile), F32),
        ),
        grid=(steps,),
        in_specs=dot_specs(mine + other, width),
        out_specs=(
            pl.BlockSpec((2, width + PAD, BLOCK), lambda n: (n, 0, 0)),
            pl.BlockSpec((1, 8, tile), lambda n: (n, 0, 0)),
        ),
        cost_estimate=COST,
        compiler_params=ROOM,
        name="h_dot",
    )(*mine, *other, w_mine, w_other)


def p_dot(mine, other, w_mine, w_other):
    width = w_mine.shape[0]
    tile = 2 * BLOCK
    return pl.pallas_call(
        p_dot_body,
        out_shape=jax.ShapeDtypeStruct((width, width), F32),
        grid=(width // tile,),
        in_specs=dot_specs((mine, other), width),
        out_specs=pl.BlockSpec((width, tile), lambda n: (0, n)),
        cost_estimate=COST,
        compiler_params=ROOM,
        name="p_dot",
    )(mine, other, w_mine, w_other)


def collect_body(source, base, *refs):
    pieces, out = refs[:-1], refs[-1]
    room = source.shape[1]
    for k, blocks in enumerate(pieces):
        for q in range(room):
            b = source[k, q]
            safe = jnp.maximum(b, 0)
            rows = pl.ds(pl.multiple_of((safe // CBLK) * BLOCK, BLOCK), BLOCK)
            cols = pl.ds(pl.multiple_of((safe % CBLK) * BLOCK, BLOCK), BLOCK)
            value = blocks[rows, cols]
            out[base[k] * room + q] = jnp.where(b >= 0, value, jnp.zeros_like(value))


def collect(pieces, source, base):
    scalar = pl.BlockSpec(memory_space=pltpu.SMEM)
    whole = pl.BlockSpec(memory_space=pltpu.VMEM)
    slots = source.shape[0] * source.shape[1]
    return pl.pallas_call(
        collect_body,
        out_shape=jax.ShapeDtypeStruct((slots, BLOCK, BLOCK), BF),
        in_specs=[scalar, scalar] + [whole] * len(pieces),
        out_specs=whole,
        compiler_params=pltpu.CompilerParams(vmem_limit_bytes=24 << 20),
        name="collect",
    )(source, base, *pieces)


def pick_body(source, blocks, out):
    for slot in range(out.shape[0]):
        k = source[slot]
        safe = jnp.maximum(k, 0)
        rows = pl.ds(pl.multiple_of((safe // CBLK) * BLOCK, BLOCK), BLOCK)
        cols = pl.ds(pl.multiple_of((safe % CBLK) * BLOCK, BLOCK), BLOCK)
        value = blocks[rows, cols]
        out[slot] = jnp.where(k >= 0, value, jnp.zeros_like(value))


def pick(blocks, source):
    slots = source.shape[0]
    return pl.pallas_call(
        pick_body,
        out_shape=jax.ShapeDtypeStruct((slots, BLOCK, BLOCK), BF),
        in_specs=[
            pl.BlockSpec(memory_space=pltpu.SMEM),
            pl.BlockSpec(memory_space=pltpu.VMEM),
        ],
        out_specs=pl.BlockSpec(memory_space=pltpu.VMEM),
        name="pick",
    )(source, blocks)


def routing(target, columns, capacity):
    count = target.shape[0]
    onehot = (target[:, None] == jnp.arange(columns, dtype=jnp.int32)[None, :]).astype(jnp.int32)
    place = jnp.arange(count, dtype=jnp.int32)
    earlier = (place[None, :] < place[:, None]).astype(jnp.int32)
    rank = jnp.sum(earlier * (target[None, :] == target[:, None]), axis=1)
    hit = (rank[:, None, None] == jnp.arange(capacity, dtype=jnp.int32)) & (onehot[:, :, None] > 0)
    return jnp.sum(jnp.where(hit, place[:, None, None] + 1, 0), axis=0) - 1


def pair_sums(derivative, blocks):
    return jnp.stack(
        [
            jnp.sum(derivative[z].astype(F32) * blocks.astype(F32), axis=(1, 2))
            for z in range(derivative.shape[0])
        ]
    )


def local(density, hamiltonian, pattern_p, pattern_h, pattern_s, owner, d_intersection, d_hamilton):
    core = lax.axis_index("core")
    columns = lax.axis_size(COL)
    slot_total = d_intersection.shape[3]
    width = CBLK * BLOCK

    capacity = slot_total // columns
    target = owner.reshape(SBLK * CBLK)
    source = routing(target, columns, capacity).reshape(slot_total)
    d_over = d_intersection.reshape(d_intersection.shape[2:])
    d_ham = d_hamilton.reshape(d_hamilton.shape[2:])

    def route(blocks):
        return exchange(pick(blocks, source), COL)

    slab = mask_slab(density, pattern_p.T, target, (SBLK * BLOCK, width))
    up, down = ([(i, (i + d) % 4) for i in range(4)] for d in (1, -1))
    barrier = lax.optimization_barrier
    height = SBLK * BLOCK
    side = flip(slab, "xhi")
    up_own = lax.ppermute(slab, "z", up)
    down_own = lax.ppermute(slab, "z", down)
    h_mine = mask(mask_body, hamiltonian, pattern_h, (width, width), 0, core)
    h_sent = mask(mask_body, hamiltonian, pattern_h, (width, width), 0, 1 - core)
    side, up_own, down_own, h_mine, h_sent = barrier((side, up_own, down_own, h_mine, h_sent))
    h_other = other_core(h_sent)
    down_side = lax.ppermute(side, "z", down)
    up_two = lax.ppermute(up_own, "z", up)
    up_side = lax.ppermute(side, "z", up)
    pieces = [slab, side, down_own, down_side, up_two, None, up_own, up_side]

    mine = [pieces[k] for k in EARLY]
    partial, peak = h_dot(mine, [other_core(v) for v in mine], h_mine, h_other)
    peak, down_side_late = barrier((peak, down_side))
    packed, down_side, up_two, density = barrier(
        (encode(partial, peak), down_side, up_two, density)
    )
    pieces[3], pieces[4], pieces[7] = down_side, up_two, up_side
    pieces[5] = lax.ppermute(down_side_late, "z", down)
    mine = [pieces[k] for k in LATE]
    packed_late = encode(*h_dot(mine, [other_core(v) for v in mine], h_mine, h_other))
    arrived, packed_late = barrier((exchange(packed, ROW_PAIR), packed_late))
    arrived_late = exchange(packed_late, ROW_PAIR)
    panel, level = decode_sum(arrived)
    panel = panel.astype(BF)
    copies = jnp.broadcast_to(panel[None], (CBLK,) + panel.shape)
    keep = jnp.repeat(jnp.repeat(pattern_s, BLOCK, axis=0), BLOCK, axis=1).astype(F32)
    p_mine = mask(turned_body, density, pattern_p.T, (width, width), core, 0)
    p_other = mask(turned_body, density, pattern_p.T, (width, width), 1 - core, 0)
    most_p = jnp.max(jnp.abs(density)).astype(F32)
    copies, arrived_late, p_mine, p_other, keep, most_p = barrier(
        (copies, arrived_late, p_mine, p_other, keep, most_p)
    )
    panel_late, level_late = decode_sum(arrived_late)
    panel_late = panel_late.astype(BF)
    copies_late = jnp.broadcast_to(panel_late[None], (CBLK,) + panel_late.shape)
    room = jnp.ceil(jnp.log2(jnp.maximum(most_p, 2.0**-100))) + 14.0
    room = jnp.full((8, BLOCK), room + jnp.maximum(level, level_late), F32)
    two = [(i, (i + 2) % 4) for i in range(4)]
    room = jnp.maximum(room, other_core(room))
    room = jnp.maximum(room, lax.ppermute(room, "z", two))
    room = jnp.maximum(room, lax.ppermute(room, "z", up))
    room = jnp.max(jnp.maximum(room, flip(room, "xhi"))) - 101.0
    room = jnp.maximum(room, -100.0)
    tiles_late, copies, room = barrier((exchange(copies_late, ROW_PAIR), copies, room))
    tiles = exchange(copies, ROW_PAIR)
    scale, unscale = jnp.exp2(14.0 - room), jnp.exp2(room - 14.0)

    part_late = p_dot(tiles_late, other_core(tiles_late), p_mine, p_other)
    blocks = {k: part_late[at * height : (at + 1) * height] * scale for at, k in enumerate(LATE)}
    near, far = lax.ppermute(blocks[4].astype(WIRE), "z", down), lax.ppermute(
        blocks[5].astype(WIRE), "z", up
    )
    tiles, near, far = barrier((tiles, near, far))
    got = [
        shifted(blocks[7].astype(WIRE), 7),
        shifted((blocks[3] + far.astype(F32)).astype(WIRE), 3),
    ]
    part = p_dot(tiles, other_core(tiles), p_mine, p_other)
    total, one, two, six = (part[at * height : (at + 1) * height] * scale for at in range(4))
    wires = [v.astype(WIRE) for v in (one, two, six + near.astype(F32))]
    total, wires = barrier((total, wires))
    last = [shifted(v, k) for v, k in zip(wires, (1, 2, 6))]
    total = barrier(total + got[0].astype(F32) + got[1].astype(F32))
    for v in last:
        total = total + v.astype(F32)
    total = total * unscale
    weighted = (total * keep).astype(BF)

    z, xhi = lax.axis_index("z"), lax.axis_index("xhi")
    step = jnp.arange(CBLK, dtype=jnp.int32)
    base = ((z + step // 2) % 4) * 2 + (xhi ^ (step % 2))
    owners = jnp.stack([p[height, : SBLK * CBLK] for p in pieces]).astype(jnp.int32)
    me = z * 2 + xhi
    found = jax.vmap(lambda t: routing(t, columns, capacity))(owners)
    mine = jnp.sum(jnp.where(jnp.arange(columns)[None, :, None] == me, found, 0), axis=1)
    routed_slab = collect(pieces, mine, base)

    first = pair_sums(d_ham, routed_slab)
    second = pair_sums(d_over, route(weighted))
    forces = (first - second) / BLOCK
    return weighted, forces.reshape((1, 1) + forces.shape)


def solution(mesh):
    fine = Mesh(mesh.devices.reshape(4, 2, 2, 4, 2), ROW + COL)
    in_specs = (
        P(COL, ROW),
        P(ROW, COL),
        P(COL, ROW),
        P(ROW, COL),
        P(COL, ROW),
        P(COL, ROW, None, None),
        P(ROW, COL, None, None, None, None),
        P(ROW, COL, None, None, None, None),
    )
    out_specs = (P(COL, ROW), P(ROW, COL, None, None))
    return jax.shard_map(local, mesh=fine, in_specs=in_specs, out_specs=out_specs, check_vma=False)
```

```python
import functools

import jax
import jax.numpy as jnp
from jax import lax
from jax.experimental import pallas as pl
from jax.experimental.pallas import tpu as pltpu
from jax.sharding import Mesh, PartitionSpec as P

BLOCK = 128
CBLK = 8
SBLK = 2
BF = jnp.bfloat16
F32 = jnp.float32
WIRE = jnp.float16
ROW = ("y", "xlo", "core")
COL = ("z", "xhi")
ROW_PAIR = ("y", "xlo")
EARLY = (0, 1, 2, 6)
LATE = (3, 7, 4, 5)
PAD = 16
TOP = 115.0


def exchange(pieces, axes):
    return lax.all_to_all(pieces, axes, split_axis=0, concat_axis=0, tiled=True)


def flip(v, axis):
    return lax.ppermute(v, axis, [(0, 1), (1, 0)])


def gather_direct(piece, axes):
    return exchange(jnp.broadcast_to(piece[None], (CBLK,) + piece.shape), axes)


def shifted(v, k):
    dz, dx = k // 2, k % 2
    nz, nx = lax.axis_size("z"), lax.axis_size("xhi")
    pairs = [
        (z * nx + x, (z + dz) % nz * nx + (x ^ dx)) for z in range(nz) for x in range(nx)
    ]
    return lax.ppermute(v, COL, pairs)


def level_of(peak):
    return jnp.ceil(jnp.log2(jnp.maximum(jnp.max(peak), 2.0**-100))) + 101.0


def encode(padded, peak):
    level = level_of(peak)
    row = lax.broadcasted_iota(jnp.int32, padded.shape, 1)
    rows = padded.shape[1] - PAD
    return jnp.where(row < rows, padded * jnp.exp2(TOP - level), level).astype(WIRE)


def decode_sum(packed):
    rows = packed.shape[1] - PAD
    factor = jnp.exp2(packed[:, rows, 0].astype(F32) - TOP)[:, None, None]
    total = jnp.sum(packed[:, :rows].astype(F32) * factor, axis=0)
    return total, jnp.max(packed[:, rows, 0].astype(F32))


def other_core(v):
    return flip(v, "core")


def keep_rows(pattern, row, col, src, dst):
    rows, cols = (size // BLOCK for size in src.shape)
    at_col = lax.broadcasted_iota(jnp.int32, (1, src.shape[1]), 1) // BLOCK
    for r in range(rows):
        keep = jnp.zeros((1, src.shape[1]), F32)
        for c in range(cols):
            keep = jnp.where(at_col == c, pattern(row + r, col + c).astype(F32), keep)
        at = slice(r * BLOCK, (r + 1) * BLOCK)
        dst[at] = src[at] * keep.astype(BF)


def mask_body(corner, pattern, src, dst):
    rows, cols = (size // BLOCK for size in src.shape)
    read = lambda r, c: pattern[r, c]
    keep_rows(read, corner[0] * rows, corner[1] * cols, src, dst)


def turned_body(corner, pattern, src, dst):
    rows, cols = (size // BLOCK for size in src.shape)
    read = lambda r, c: pattern[c, r]
    keep_rows(read, corner[0] * rows, corner[1] * cols, src, dst)


def slab_body(target, pattern, src, dst):
    rows, cols = src.shape
    keep_rows(lambda r, c: pattern[c, r], 0, 0, src, dst.at[:rows])
    lane = lax.broadcasted_iota(jnp.int32, (PAD, cols), 1)
    note = jnp.zeros((PAD, cols), F32)
    for k in range(SBLK * CBLK):
        note = jnp.where(lane == k, target[k].astype(F32), note)
    dst[rows:] = note.astype(BF)


def call_mask(body, scalars, matrix, shape, height, index):
    return pl.pallas_call(
        body,
        out_shape=jax.ShapeDtypeStruct((height, shape[1]), BF),
        grid_spec=pltpu.PrefetchScalarGridSpec(
            num_scalar_prefetch=2,
            grid=(1,),
            in_specs=[pl.BlockSpec(shape, index)],
            out_specs=pl.BlockSpec((height, shape[1]), lambda g, at, pat: (0, 0)),
        ),
        name=body.__name__,
    )(*scalars, matrix)


def mask(body, matrix, pattern, shape, row, col):
    corner = jnp.stack((jnp.asarray(row, jnp.int32), jnp.asarray(col, jnp.int32)))
    index = lambda g, at, pat: (at[0], at[1])
    return call_mask(body, (corner, pattern), matrix, shape, shape[0], index)


def mask_slab(matrix, pattern, target, shape):
    index = lambda g, at, pat: (0, 0)
    return call_mask(slab_body, (target, pattern), matrix, shape, shape[0] + PAD, index)


def h_dot_body(*refs):
    count = (len(refs) - 4) // 2
    mine, other = refs[:count], refs[count : 2 * count]
    w_mine, w_other, out, peak = refs[2 * count :]
    height = mine[0].shape[0] - PAD
    tops = []
    for at in range(count):
        values = jnp.dot(mine[at][:height], w_mine[...], preferred_element_type=F32)
        values += jnp.dot(other[at][:height], w_other[...], preferred_element_type=F32)
        for g in range(out.shape[0]):
            out[g, at * height : (at + 1) * height] = values[:, g * BLOCK : (g + 1) * BLOCK]
        tops.append(jnp.max(jnp.abs(values), axis=0, keepdims=True))
    for g in range(out.shape[0]):
        out[g, count * height :] = jnp.zeros((PAD, BLOCK), F32)
    peak[0] = jnp.broadcast_to(functools.reduce(jnp.maximum, tops), peak.shape[1:])


def p_dot_body(mine, other, w_mine, w_other, out):
    def flat(tiles):
        return jnp.concatenate([tiles[g] for g in range(CBLK)], axis=1)

    values = jnp.dot(flat(mine), w_mine[...], preferred_element_type=F32)
    values += jnp.dot(flat(other), w_other[...], preferred_element_type=F32)
    out[...] = values


COST = pl.CostEstimate(flops=1 << 20, bytes_accessed=1 << 20, transcendentals=0)
ROOM = pltpu.CompilerParams(vmem_limit_bytes=58 << 20)


def dot_specs(operands, width):
    whole = [pl.BlockSpec(v.shape, lambda n, rank=v.ndim: (0,) * rank) for v in operands]
    return whole + [pl.BlockSpec((width, 4 * BLOCK), lambda n: (0, n))] * 2


def h_dot(mine, other, w_mine, w_other):
    width = w_mine.shape[0]
    tile = 4 * BLOCK
    steps = width // tile
    return pl.pallas_call(
        h_dot_body,
        out_shape=(
            jax.ShapeDtypeStruct((CBLK, width + PAD, BLOCK), F32),
            jax.ShapeDtypeStruct((steps, 8, tile), F32),
        ),
        grid=(steps,),
        in_specs=dot_specs(mine + other, width),
        out_specs=(
            pl.BlockSpec((4, width + PAD, BLOCK), lambda n: (n, 0, 0)),
            pl.BlockSpec((1, 8, tile), lambda n: (n, 0, 0)),
        ),
        cost_estimate=COST,
        compiler_params=ROOM,
        name="h_dot",
    )(*[pltpu.with_memory_space_constraint(v, pltpu.HBM) for v in (*mine, *other, w_mine, w_other)])


def p_dot(mine, other, w_mine, w_other):
    width = w_mine.shape[0]
    tile = 4 * BLOCK
    return pl.pallas_call(
        p_dot_body,
        out_shape=jax.ShapeDtypeStruct((width, width), F32),
        grid=(width // tile,),
        in_specs=dot_specs((mine, other), width),
        out_specs=pl.BlockSpec((width, tile), lambda n: (0, n)),
        cost_estimate=COST,
        compiler_params=ROOM,
        name="p_dot",
    )(mine, other, w_mine, w_other)


def collect_body(source, base, *refs):
    pieces, out = refs[:-1], refs[-1]
    room = source.shape[1]
    for k, blocks in enumerate(pieces):
        for q in range(room):
            b = source[k, q]
            safe = jnp.maximum(b, 0)
            rows = pl.ds(pl.multiple_of((safe // CBLK) * BLOCK, BLOCK), BLOCK)
            cols = pl.ds(pl.multiple_of((safe % CBLK) * BLOCK, BLOCK), BLOCK)
            value = blocks[rows, cols]
            out[base[k] * room + q] = jnp.where(b >= 0, value, jnp.zeros_like(value))


def collect(pieces, source, base):
    scalar = pl.BlockSpec(memory_space=pltpu.SMEM)
    whole = pl.BlockSpec(memory_space=pltpu.VMEM)
    slots = source.shape[0] * source.shape[1]
    return pl.pallas_call(
        collect_body,
        out_shape=jax.ShapeDtypeStruct((slots, BLOCK, BLOCK), BF),
        in_specs=[scalar, scalar] + [whole] * len(pieces),
        out_specs=whole,
        compiler_params=pltpu.CompilerParams(vmem_limit_bytes=24 << 20),
        name="collect",
    )(source, base, *pieces)


def pick_body(source, blocks, out):
    for slot in range(out.shape[0]):
        k = source[slot]
        safe = jnp.maximum(k, 0)
        rows = pl.ds(pl.multiple_of((safe // CBLK) * BLOCK, BLOCK), BLOCK)
        cols = pl.ds(pl.multiple_of((safe % CBLK) * BLOCK, BLOCK), BLOCK)
        value = blocks[rows, cols]
        out[slot] = jnp.where(k >= 0, value, jnp.zeros_like(value))


def pick(blocks, source):
    slots = source.shape[0]
    return pl.pallas_call(
        pick_body,
        out_shape=jax.ShapeDtypeStruct((slots, BLOCK, BLOCK), BF),
        in_specs=[
            pl.BlockSpec(memory_space=pltpu.SMEM),
            pl.BlockSpec(memory_space=pltpu.VMEM),
        ],
        out_specs=pl.BlockSpec(memory_space=pltpu.VMEM),
        name="pick",
    )(source, blocks)


def routing(target, columns, capacity):
    count = target.shape[0]
    onehot = (target[:, None] == jnp.arange(columns, dtype=jnp.int32)[None, :]).astype(jnp.int32)
    place = jnp.arange(count, dtype=jnp.int32)
    earlier = (place[None, :] < place[:, None]).astype(jnp.int32)
    rank = jnp.sum(earlier * (target[None, :] == target[:, None]), axis=1)
    hit = (rank[:, None, None] == jnp.arange(capacity, dtype=jnp.int32)) & (onehot[:, :, None] > 0)
    return jnp.sum(jnp.where(hit, place[:, None, None] + 1, 0), axis=0) - 1


def pair_sums(derivative, blocks):
    return jnp.stack(
        [
            jnp.sum(derivative[z].astype(F32) * blocks.astype(F32), axis=(1, 2))
            for z in range(derivative.shape[0])
        ]
    )


def local(density, hamiltonian, pattern_p, pattern_h, pattern_s, owner, d_intersection, d_hamilton):
    core = lax.axis_index("core")
    columns = lax.axis_size(COL)
    slot_total = d_intersection.shape[3]
    width = CBLK * BLOCK

    capacity = slot_total // columns
    target = owner.reshape(SBLK * CBLK)
    source = routing(target, columns, capacity).reshape(slot_total)
    d_over = d_intersection.reshape(d_intersection.shape[2:])
    d_ham = d_hamilton.reshape(d_hamilton.shape[2:])

    def route(blocks):
        return exchange(pick(blocks, source), COL)

    slab = mask_slab(density, pattern_p.T, target, (SBLK * BLOCK, width))
    up, down = ([(i, (i + d) % 4) for i in range(4)] for d in (1, -1))
    barrier = lax.optimization_barrier
    height = SBLK * BLOCK
    side = flip(slab, "xhi")
    up_own = lax.ppermute(slab, "z", up)
    down_own = lax.ppermute(slab, "z", down)
    h_mine = mask(mask_body, hamiltonian, pattern_h, (width, width), 0, core)
    h_sent = mask(mask_body, hamiltonian, pattern_h, (width, width), 0, 1 - core)
    side, up_own, down_own, h_mine, h_sent = barrier((side, up_own, down_own, h_mine, h_sent))
    h_other = other_core(h_sent)
    down_side = lax.ppermute(side, "z", down)
    up_two = lax.ppermute(up_own, "z", up)
    up_side = lax.ppermute(side, "z", up)
    pieces = [slab, side, down_own, down_side, up_two, None, up_own, up_side]

    mine = [pieces[k] for k in EARLY]
    partial, peak = h_dot(mine, [other_core(v) for v in mine], h_mine, h_other)
    peak, down_side_late = barrier((peak, down_side))
    packed, down_side, up_two, density = barrier(
        (encode(partial, peak), down_side, up_two, density)
    )
    pieces[3], pieces[4], pieces[7] = down_side, up_two, up_side
    pieces[5] = lax.ppermute(down_side_late, "z", down)
    mine = [pieces[k] for k in LATE]
    packed_late = encode(*h_dot(mine, [other_core(v) for v in mine], h_mine, h_other))
    arrived, packed_late = barrier((exchange(packed, ROW_PAIR), packed_late))
    arrived_late = exchange(packed_late, ROW_PAIR)
    panel, level = decode_sum(arrived)
    panel = panel.astype(BF)
    copies = jnp.broadcast_to(panel[None], (CBLK,) + panel.shape)
    keep = jnp.repeat(jnp.repeat(pattern_s, BLOCK, axis=0), BLOCK, axis=1).astype(F32)
    p_mine = mask(turned_body, density, pattern_p.T, (width, width), core, 0)
    p_other = mask(turned_body, density, pattern_p.T, (width, width), 1 - core, 0)
    most_p = jnp.max(jnp.abs(density)).astype(F32)
    copies, arrived_late, p_mine, p_other, keep, most_p = barrier(
        (copies, arrived_late, p_mine, p_other, keep, most_p)
    )
    panel_late, level_late = decode_sum(arrived_late)
    panel_late = panel_late.astype(BF)
    copies_late = jnp.broadcast_to(panel_late[None], (CBLK,) + panel_late.shape)
    room = jnp.ceil(jnp.log2(jnp.maximum(most_p, 2.0**-100))) + 14.0
    room = jnp.full((8, BLOCK), room + jnp.maximum(level, level_late), F32)
    two = [(i, (i + 2) % 4) for i in range(4)]
    room = jnp.maximum(room, other_core(room))
    room = jnp.maximum(room, lax.ppermute(room, "z", two))
    room = jnp.maximum(room, lax.ppermute(room, "z", up))
    room = jnp.max(jnp.maximum(room, flip(room, "xhi"))) - 101.0
    room = jnp.maximum(room, -100.0)
    tiles_late, copies, room = barrier((exchange(copies_late, ROW_PAIR), copies, room))
    tiles = exchange(copies, ROW_PAIR)
    scale, unscale = jnp.exp2(14.0 - room), jnp.exp2(room - 14.0)

    part_late = p_dot(tiles_late, other_core(tiles_late), p_mine, p_other)
    blocks = {k: part_late[at * height : (at + 1) * height] * scale for at, k in enumerate(LATE)}
    near, far = lax.ppermute(blocks[4].astype(WIRE), "z", down), lax.ppermute(
        blocks[5].astype(WIRE), "z", up
    )
    tiles, near, far = barrier((tiles, near, far))
    got = [
        shifted(blocks[7].astype(WIRE), 7),
        shifted((blocks[3] + far.astype(F32)).astype(WIRE), 3),
    ]
    part = p_dot(tiles, other_core(tiles), p_mine, p_other)
    total, one, two, six = (part[at * height : (at + 1) * height] * scale for at in range(4))
    wires = [v.astype(WIRE) for v in (one, two, six + near.astype(F32))]
    total, wires = barrier((total, wires))
    last = [shifted(v, k) for v, k in zip(wires, (1, 2, 6))]
    total = barrier(total + got[0].astype(F32) + got[1].astype(F32))
    for v in last:
        total = total + v.astype(F32)
    total = total * unscale
    weighted = (total * keep).astype(BF)

    z, xhi = lax.axis_index("z"), lax.axis_index("xhi")
    step = jnp.arange(CBLK, dtype=jnp.int32)
    base = ((z + step // 2) % 4) * 2 + (xhi ^ (step % 2))
    owners = jnp.stack([p[height, : SBLK * CBLK] for p in pieces]).astype(jnp.int32)
    me = z * 2 + xhi
    found = jax.vmap(lambda t: routing(t, columns, capacity))(owners)
    mine = jnp.sum(jnp.where(jnp.arange(columns)[None, :, None] == me, found, 0), axis=1)
    routed_slab = collect(pieces, mine, base)

    first = pair_sums(d_ham, routed_slab)
    second = pair_sums(d_over, route(weighted))
    forces = (first - second) / BLOCK
    return weighted, forces.reshape((1, 1) + forces.shape)


def solution(mesh):
    fine = Mesh(mesh.devices.reshape(4, 2, 2, 4, 2), ROW + COL)
    in_specs = (
        P(COL, ROW),
        P(ROW, COL),
        P(COL, ROW),
        P(ROW, COL),
        P(COL, ROW),
        P(COL, ROW, None, None),
        P(ROW, COL, None, None, None, None),
        P(ROW, COL, None, None, None, None),
    )
    out_specs = (P(COL, ROW), P(ROW, COL, None, None))
    return jax.shard_map(local, mesh=fine, in_specs=in_specs, out_specs=out_specs, check_vma=False)
```
